512 devices in a mesh: tmpl: 8 (over x, y_hi), freq: 64 (over z, y_lo, core).
Axes of the slice: x: 4, y: 8 (y_hi: 2, y_lo: 4; y = y_hi * 4 + y_lo), z: 8, core: 2. Of those that a mesh axis runs over, the one named last changes fastest.
Arguments:
- strain: float32 [512, 512], P('freq'), may hold values from -6 to 6
- inv_asd: float32 [512, 512], P('freq'), may hold values from 0.25 to 4
- spectra: bfloat16 [512, 64, 2, 512], P('freq', 'tmpl'), may hold values from -6 to 6
- cutoff: int32 [64], P('tmpl'), may hold values from 64 to 256
Outputs:
- filter_series: float32 [64, 2, 512, 512], P('tmpl', None, 'freq')
- peak_power: float32 [512, 512], P('freq')
The draws below stay inside these ranges and needn't reach their ends.
All inputs are finite; a program needn't handle non-finite values.
Results may differ from the reference program's by a relative error of at most 0.0051.
Values may be sent and summed in bfloat16 or wider, within the bound.
A program may use at most 64 MiB of HBM per device.

```python
import math
import jax
import jax.numpy as jnp
from jax import lax

N1 = 512
TEMPLATES = 64


def with_ends(result, stream_key, low, top_value):
    longest = result.shape.index(max(result.shape))
    spots = []
    for shift in (0, 1):
        where = [jax.random.randint(jax.random.fold_in(stream_key, axis), (), 0, length) for axis, length in enumerate(result.shape)]
        where[longest] = (where[longest] + shift) % result.shape[longest]
        spots.append(tuple(where))
    return result.at[spots[0]].set(low).at[spots[1]].set(top_value)


def block_levels(rng, shape, split, low, top_value):
    def one(position, blocks):
        draws = jax.random.uniform(jax.random.fold_in(jax.random.fold_in(rng, 6), position), (blocks,), jnp.float32, low / len(split), top_value / len(split))
        return jnp.repeat(jnp.exp(draws), shape[position] // blocks).reshape((-1,) + (1,) * (len(shape) - position - 1))

    level = one(*split[0])
    for cut in split[1:]:
        level = level * one(*cut)
    return level


def bell_draw(rng, extent, width, limit, shards=(), held_as=jnp.bfloat16):
    array = width * jax.random.normal(rng, extent, jnp.float32)
    if shards:
        array = array * block_levels(rng, extent, shards, -0.22, 0.18)
    return jnp.clip(array, -limit, limit).astype(held_as)


def setup_inputs(seed: int = 0) -> dict:
    streams_of = jax.random.split(jax.random.key(seed), 5)
    return {
        "strain": bell_draw(streams_of[0], (N1, N1), 1.0, 6.0, ((0, 64),), jnp.float32),
        "inv_asd": jnp.clip(jnp.exp(math.log(4.0) - 2.7725887 * jax.random.uniform(streams_of[1], (N1, N1), jnp.float32) ** block_levels(streams_of[1], (N1, N1), ((0, 64),), -0.2, 0.2)), 0.25, 4.0),
        "spectra": bell_draw(streams_of[2], (N1, TEMPLATES, 2, N1), 1.0, 6.0, ((0, 64), (1, 8))),
        "cutoff": with_ends(jax.random.randint(streams_of[3], (TEMPLATES,), N1 // 8, N1 // 2 + 1), jax.random.fold_in(streams_of[3], 1), N1 // 8, (N1 // 2 + 1) - 1).astype(jnp.int32),
    }


def angle_table(left, right, modulus):
    product = (left[:, None] * right[None, :]) % modulus
    return (2.0 * math.pi / modulus) * product.astype(jnp.float32)


def inverse_table(side_size):
    positions = jnp.arange(side_size, dtype=jnp.int32)
    angles = angle_table(positions, positions, side_size)
    cosines = jnp.cos(angles)
    sine_part = jnp.sin(angles)
    stacked = jnp.stack([jnp.stack([cosines, sine_part]), jnp.stack([-sine_part, cosines])])
    return stacked.astype(jnp.bfloat16)


def reference(strain, inv_asd, spectra, cutoff):
    side_size = N1
    total_size = side_size * side_size
    spectrum_full = jnp.fft.fft(strain.reshape(-1)).reshape(side_size, side_size).T
    white_real = jnp.real(spectrum_full).astype(jnp.float32) * inv_asd
    white_imag = jnp.imag(spectrum_full).astype(jnp.float32) * inv_asd
    base_table = inverse_table(side_size)
    section_table = jnp.transpose(base_table, (0, 2, 1, 3)).astype(jnp.float32)
    last_table = jnp.transpose(base_table, (2, 0, 1, 3)).astype(jnp.float32)
    positions = jnp.arange(side_size, dtype=jnp.int32)
    twist_angle = angle_table(positions, positions, total_size)
    twist_cos = jnp.cos(twist_angle)[:, :, None]
    twist_sin = jnp.sin(twist_angle)[:, :, None]
    group_size = math.gcd(8, TEMPLATES)

    def one_block(peak_power, block_index):
        chosen = lax.dynamic_slice_in_dim(spectra, block_index * group_size, group_size, 1).astype(jnp.float32)
        limits = lax.dynamic_slice_in_dim(cutoff, block_index * group_size, group_size, 0)
        band_mask = (positions[None, :] < limits[:, None]).astype(jnp.float32)[None]
        spec_real = chosen[:, :, 0]
        spec_imag = chosen[:, :, 1]
        prod_real = (white_real[:, None] * spec_real + white_imag[:, None] * spec_imag) * band_mask
        prod_imag = (white_imag[:, None] * spec_real - white_real[:, None] * spec_imag) * band_mask
        product = jnp.stack([prod_real, prod_imag], 2).astype(jnp.bfloat16)
        turned = jnp.einsum("ktcj,cjdm->kmtd", product.astype(jnp.float32), section_table)
        real_part = turned[..., 0]
        imag_part = turned[..., 1]
        rotated = jnp.stack([real_part * twist_cos - imag_part * twist_sin, real_part * twist_sin + imag_part * twist_cos], -1).astype(jnp.bfloat16)
        series = jnp.einsum("kmtc,kcdn->tdmn", rotated.astype(jnp.float32), last_table) * (1.0 / total_size)
        power_sum = series[:, 0] ** 2 + series[:, 1] ** 2
        return jnp.maximum(peak_power, jnp.max(power_sum, axis=0)), series

    start_peak = jnp.zeros((side_size, side_size), jnp.float32)
    peak_power, blocks = lax.scan(one_block, start_peak, jnp.arange(TEMPLATES // group_size, dtype=jnp.int32))
    filter_series = blocks.reshape(TEMPLATES, 2, side_size, side_size)
    return filter_series, peak_power
```

```python
import functools
import math

import jax
import jax.numpy as jnp
import numpy as np
from jax import lax
from jax.experimental import pallas as pl
from jax.experimental.pallas import tpu as pltpu
from jax.sharding import PartitionSpec as P

SIDE = 512
BAND = 256
TOTAL = SIDE * SIDE
NZ = 8
NY = 4
NC = 2
NW = NY * NC
NX = 4
NH = 2
NF = NZ * NW
ROWS = SIDE // NF
TEMPL = 8
PAIRS = 2 * TEMPL
MESH = pl.DeviceIdType.MESH
F32 = jnp.float32
BF16 = jnp.bfloat16


def base_tables():
    index = np.arange(SIDE)
    angle = 2.0 * np.pi / SIDE * (np.outer(index, index) % SIDE)
    cosines = np.cos(angle).astype(np.float32)
    sines = np.sin(angle).astype(np.float32)
    whole = np.concatenate([cosines, sines], 1)
    high = whole.astype(jnp.bfloat16)
    part = np.concatenate([cosines[:, :BAND], sines[:, :BAND]], 1)
    low = (part - part.astype(jnp.bfloat16).astype(np.float32)).astype(jnp.bfloat16)
    return high, low


def iota(shape, axis):
    return lax.broadcasted_iota(jnp.int32, shape, axis)


def dot(left, right):
    return jnp.dot(left, right, preferred_element_type=F32)


def split(value):
    high = value.astype(BF16)
    return high, (value - high.astype(F32)).astype(BF16)


def regroup(values):
    lane = iota((ROWS, 128), 1)
    for bit in range(4):
        low = 1 << bit
        width = ROWS * low
        keep = (lane & width) == 0
        moved = list(values)
        for first in range(PAIRS):
            if first & low:
                continue
            second = first | low
            moved[first] = jnp.where(keep, values[first], pltpu.roll(values[second], width, 1))
            moved[second] = jnp.where(keep, pltpu.roll(values[first], 128 - width, 1), values[second])
        values = moved
    return values


def kernel(
    strain, inv_asd, spectra, cutoff, high_table, low_table, series, peak,
    table, table_low, strain_v, asd_v, spectra_v, cut_s, gathered, partial, partials,
    weights, outgoing, received, best, bests, best_half, other_half,
    load_sem, z_send, z_recv, w_send, w_recv, done_sem, f_send, f_recv, x_send, x_recv, h_send, h_recv,
):
    me_t = lax.axis_index("tmpl")
    me_f = lax.axis_index("freq")
    z_pos = me_f // NW
    w_pos = me_f % NW
    core = me_f % NC
    x_pos = me_t // NH
    half = me_t % NH
    y_full = half * NY + w_pos // NC

    loads = [
        pltpu.make_async_copy(strain, strain_v, load_sem.at[0]),
        pltpu.make_async_copy(spectra.at[:, :, :, pl.ds(0, BAND)], spectra_v, load_sem.at[1]),
        pltpu.make_async_copy(inv_asd.at[:, pl.ds(0, BAND)], asd_v, load_sem.at[2]),
        pltpu.make_async_copy(cutoff, cut_s, load_sem.at[3]),
        pltpu.make_async_copy(high_table, table, load_sem.at[4]),
        pltpu.make_async_copy(low_table, table_low, load_sem.at[5]),
    ]
    for load in loads:
        load.start()

    barrier = pltpu.get_barrier_semaphore()

    def greet(device):
        pl.semaphore_signal(barrier, inc=1, device_id=device, device_id_type=MESH)

    for step in range(1, NZ):
        greet((me_t, (z_pos + step) % NZ * NW + w_pos))
    columns = NH * NY * NC
    for step in range(1, columns):
        place = (y_full * NC + core + step) % columns
        greet((x_pos * NH + place // NW, z_pos * NW + place % NW))
    for step in range(1, NX):
        greet(((x_pos + step) % NX * NH + half, me_f))

    loads[0].wait()
    own = strain_v[...]
    gathered[z_pos] = jnp.concatenate([own[:, :BAND], own[:, BAND:]], 0).astype(BF16)

    pl.semaphore_wait(barrier, NZ - 1 + columns - 1 + NX - 1)

    z_copies = []
    for step in range(1, NZ):
        copy = pltpu.make_async_remote_copy(
            src_ref=gathered.at[z_pos], dst_ref=gathered.at[z_pos], send_sem=z_send, recv_sem=z_recv,
            device_id=(me_t, (z_pos + step) % NZ * NW + w_pos), device_id_type=MESH,
        )
        copy.start()

    row = iota((128, 128), 0)
    col = iota((128, 128), 1)
    freq_row = 64 * z_pos + 8 * (row // 16) + row % 8
    sample_row = 64 * (col // 16) + 8 * w_pos + col % 8
    turns = (freq_row * sample_row + 128 * (row // 8 % 2)) & (SIDE - 1)
    first = jnp.cos(turns.astype(F32) * (2.0 * math.pi / SIDE))
    side = col // 8 % 2
    first = jnp.concatenate([jnp.where(side == 0, first, 0.0), jnp.where(side == 1, first, 0.0)], 0)
    first_high, first_low = split(first)
    twist = (ROWS * me_f + iota((ROWS, SIDE), 0)) * iota((ROWS, SIDE), 1)
    twist = twist.astype(F32) * (2.0 * math.pi / TOTAL)
    twist_cos = jnp.cos(twist)
    twist_sin = jnp.sin(twist)

    loads[1].wait()
    loads[2].wait()
    loads[3].wait()
    wanted = row % 8 * PAIRS + row // 8 % 8 * 2 + row // 64
    order = jnp.where(col == wanted, 1.0, 0.0).astype(BF16)
    sorted_spectra = dot(order, spectra_v[...].reshape(128, BAND))
    scale = asd_v[...]
    lane = iota((ROWS, BAND), 1)
    for templ in range(TEMPL):
        gain = jnp.where(lane < cut_s[templ], scale, 0.0)
        for part in range(2):
            block = slice((part * TEMPL + templ) * ROWS, (part * TEMPL + templ + 1) * ROWS)
            weights[block, :] = sorted_spectra[block, :] * gain

    pltpu.make_async_copy(gathered.at[pl.ds(0, NZ - 1)], gathered.at[pl.ds(0, NZ - 1)], z_recv).wait()
    for step in range(1, NW):
        pl.semaphore_signal(
            done_sem, inc=1, device_id=(me_t, z_pos * NW + (w_pos + step) % NW), device_id_type=MESH
        )
    blocks = gathered[...].reshape(128, BAND)
    shares = dot(first_high, blocks) + dot(first_low, blocks)
    partial[:, :, :BAND] = shares[:128].reshape(NW, 16, BAND).astype(BF16)
    partial[:, :, BAND:] = shares[128:].reshape(NW, 16, BAND).astype(BF16)
    for step in range(NY):
        for to_core in range(NC):
            if step == 2:
                away = 2 if to_core == 0 else 6
            else:
                away = (0, 1, 2, 7)[step]
            place = (y_full + away) % (NH * NY)
            target_core = to_core
            target_w = place % NY * NC + target_core
            if step == 0:
                if to_core == 0:
                    continue
                target_w = w_pos // NC * NC + (1 - core)
            copy = pltpu.make_async_remote_copy(
                src_ref=partial.at[target_w], dst_ref=partials.at[w_pos], send_sem=w_send, recv_sem=w_recv,
                device_id=(x_pos * NH + place // NY, z_pos * NW + target_w), device_id_type=MESH,
            )
            copy.start()
    partials[w_pos] = partial[w_pos]
    pltpu.make_async_copy(partials.at[pl.ds(0, NW - 1)], partials.at[pl.ds(0, NW - 1)], w_recv).wait()
    sums = partials[0].astype(F32)
    for slot in range(1, NW):
        sums = sums + partials[slot].astype(F32)
    sum_real = sums[:ROWS]
    sum_imag = sums[ROWS:]
    turned = jnp.concatenate(
        [sum_real * twist_cos + sum_imag * twist_sin, sum_imag * twist_cos - sum_real * twist_sin], 0
    )
    turned_high, turned_low = split(turned)

    loads[4].wait()
    loads[5].wait()
    both = jnp.concatenate([turned_high, turned_low], 0)
    by_cos = dot(both, table[:, :BAND])
    by_sin = dot(both, table[:, SIDE : SIDE + BAND])
    by_cos = by_cos[:16] + by_cos[16:] + dot(turned_high, table_low[:, :BAND])
    by_sin = by_sin[:16] + by_sin[16:] + dot(turned_high, table_low[:, BAND:])
    spec_real = by_cos[:ROWS] + by_sin[ROWS:]
    spec_imag = by_cos[ROWS:] - by_sin[:ROWS]

    product = []
    for templ in range(TEMPL):
        gain_real = weights[templ * ROWS : (templ + 1) * ROWS, :]
        gain_imag = weights[(TEMPL + templ) * ROWS : (TEMPL + templ + 1) * ROWS, :]
        product.append(spec_real * gain_real + spec_imag * gain_imag)
    for templ in range(TEMPL):
        gain_real = weights[templ * ROWS : (templ + 1) * ROWS, :]
        gain_imag = weights[(TEMPL + templ) * ROWS : (TEMPL + templ + 1) * ROWS, :]
        product.append(spec_imag * gain_real - spec_real * gain_imag)
    product = jnp.concatenate(product, 0).astype(BF16)

    pl.semaphore_wait(done_sem, NW - 1)
    for pair in range(2):
        start = pair * 256
        by_cos = dot(product, table[:BAND, start : start + 256])
        by_sin = dot(product, table[:BAND, SIDE + start : SIDE + start + 256])
        for inner in range(2):
            column = 2 * pair + inner
            here = slice(inner * 128, (inner + 1) * 128)
            cos_here = twist_cos[:, column * 128 : (column + 1) * 128]
            sin_here = twist_sin[:, column * 128 : (column + 1) * 128]
            reals = []
            imags = []
            for templ in range(TEMPL):
                up = slice(templ * ROWS, (templ + 1) * ROWS)
                down = slice((TEMPL + templ) * ROWS, (TEMPL + templ + 1) * ROWS)
                real_part = by_cos[up, here] - by_sin[down, here]
                imag_part = by_sin[up, here] + by_cos[down, here]
                reals.append(real_part * cos_here - imag_part * sin_here)
                imags.append(real_part * sin_here + imag_part * cos_here)
            for slot, tile in enumerate(regroup(reals + imags)):
                outgoing[column * 16 + slot] = tile.astype(BF16)

    def send(step, carry):
        target = (me_f + step) % NF
        pltpu.make_async_remote_copy(
            src_ref=outgoing.at[target], dst_ref=received.at[me_f], send_sem=f_send, recv_sem=f_recv,
            device_id=(me_t, target), device_id_type=MESH,
        ).start()
        return carry

    lax.fori_loop(1, NF, send, 0)
    received[me_f] = outgoing[me_f]
    pltpu.make_async_copy(received.at[pl.ds(0, NF - 1)], received.at[pl.ds(0, NF - 1)], f_recv).wait()

    columns_in = jnp.transpose(received[...].reshape(SIDE, 128))
    for pair in range(2):
        start = pair * 256
        by_cos = dot(columns_in, table[:, start : start + 256]) * (1.0 / TOTAL)
        by_sin = dot(columns_in, table[:, SIDE + start : SIDE + start + 256]) * (1.0 / TOTAL)
        top = None
        for templ in range(TEMPL):
            up = slice(templ * ROWS, (templ + 1) * ROWS)
            down = slice((TEMPL + templ) * ROWS, (TEMPL + templ + 1) * ROWS)
            real_part = by_cos[up] - by_sin[down]
            imag_part = by_sin[up] + by_cos[down]
            series[templ, 0, :, start : start + 256] = real_part
            series[templ, 1, :, start : start + 256] = imag_part
            power = real_part * real_part + imag_part * imag_part
            top = power if top is None else jnp.maximum(top, power)
        best[:, start : start + 256] = top

    for step in range(1, NX):
        pltpu.make_async_remote_copy(
            src_ref=best, dst_ref=bests.at[x_pos], send_sem=x_send, recv_sem=x_recv,
            device_id=((x_pos + step) % NX * NH + half, me_f), device_id_type=MESH,
        ).start()
    bests[x_pos] = best[...]
    pltpu.make_async_copy(bests.at[pl.ds(0, NX - 1)], bests.at[pl.ds(0, NX - 1)], x_recv).wait()
    top = jnp.maximum(jnp.maximum(bests[0], bests[1]), jnp.maximum(bests[2], bests[3]))
    best_half[...] = top
    last = pltpu.make_async_remote_copy(
        src_ref=best_half, dst_ref=other_half, send_sem=h_send, recv_sem=h_recv,
        device_id=(x_pos * NH + 1 - half, me_f), device_id_type=MESH,
    )
    last.start()
    last.wait()
    peak[...] = jnp.maximum(top, other_half[...])

    pltpu.make_async_copy(gathered.at[pl.ds(0, NZ - 1)], gathered.at[pl.ds(0, NZ - 1)], z_send).wait()
    pltpu.make_async_copy(partial.at[pl.ds(0, NW - 1)], partial.at[pl.ds(0, NW - 1)], w_send).wait()
    pltpu.make_async_copy(outgoing.at[pl.ds(0, NF - 1)], outgoing.at[pl.ds(0, NF - 1)], f_send).wait()
    pltpu.make_async_copy(bests.at[pl.ds(0, NX - 1)], bests.at[pl.ds(0, NX - 1)], x_send).wait()


def local(strain, inv_asd, spectra, cutoff):
    high, low = base_tables()
    anywhere = pl.BlockSpec(memory_space=pl.ANY)
    inside = pl.BlockSpec(memory_space=pltpu.VMEM)
    dma = pltpu.SemaphoreType.DMA
    return pl.pallas_call(
        kernel,
        out_shape=(
            jax.ShapeDtypeStruct((TEMPL, 2, ROWS, SIDE), F32),
            jax.ShapeDtypeStruct((ROWS, SIDE), F32),
        ),
        in_specs=[anywhere] * 6,
        out_specs=(inside, inside),
        scratch_shapes=[
            pltpu.VMEM((SIDE, 2 * SIDE), BF16),
            pltpu.VMEM((SIDE, SIDE), BF16),
            pltpu.VMEM((ROWS, SIDE), F32),
            pltpu.VMEM((ROWS, BAND), F32),
            pltpu.VMEM((ROWS, TEMPL, 2, BAND), BF16),
            pltpu.SMEM((TEMPL,), jnp.int32),
            pltpu.VMEM((NZ, 16, BAND), BF16),
            pltpu.VMEM((NW, 16, SIDE), BF16),
            pltpu.VMEM((NW, 16, SIDE), BF16),
            pltpu.VMEM((128, BAND), F32),
            pltpu.VMEM((NF, ROWS, 128), BF16),
            pltpu.VMEM((NF, ROWS, 128), BF16),
            pltpu.VMEM((ROWS, SIDE), F32),
            pltpu.VMEM((NX, ROWS, SIDE), F32),
            pltpu.VMEM((ROWS, SIDE), F32),
            pltpu.VMEM((ROWS, SIDE), F32),
            dma((6,)), dma, dma, dma, dma, pltpu.SemaphoreType.REGULAR, dma, dma, dma, dma, dma, dma,
        ],
        compiler_params=pltpu.CompilerParams(collective_id=0, has_side_effects=True),
    )(strain, inv_asd, spectra, cutoff, jnp.asarray(high), jnp.asarray(low))


def solution(mesh):
    in_specs = (P("freq", None), P("freq", None), P("freq", "tmpl", None, None), P("tmpl"))
    out_specs = (P("tmpl", None, "freq", None), P("freq", None))
    return jax.shard_map(local, mesh=mesh, in_specs=in_specs, out_specs=out_specs, check_vma=False)
```

```python
import functools
import math

import jax
import jax.numpy as jnp
import numpy as np
from jax import lax
from jax.experimental import pallas as pl
from jax.experimental.pallas import tpu as pltpu
from jax.sharding import PartitionSpec as P

SIDE = 512
BAND = 256
TOTAL = SIDE * SIDE
NZ = 8
NY = 4
NC = 2
NW = NY * NC
NX = 4
NH = 2
NF = NZ * NW
ROWS = SIDE // NF
TEMPL = 8
PAIRS = 2 * TEMPL
FAR_FIRST = (4, 3, 5, 2, 6, 1, 7)
MESH = pl.DeviceIdType.MESH
F32 = jnp.float32
BF16 = jnp.bfloat16


def base_tables():
    index = np.arange(SIDE)
    angle = 2.0 * np.pi / SIDE * (np.outer(index, index) % SIDE)
    cosines = np.cos(angle).astype(np.float32)
    sines = np.sin(angle).astype(np.float32)
    whole = np.concatenate([cosines, sines], 1)
    high = whole.astype(jnp.bfloat16)
    part = np.concatenate([cosines[:, :BAND], sines[:, :BAND]], 1)
    low = (part - part.astype(jnp.bfloat16).astype(np.float32)).astype(jnp.bfloat16)
    return high, low


def iota(shape, axis):
    return lax.broadcasted_iota(jnp.int32, shape, axis)


def dot(left, right):
    return jnp.dot(left, right, preferred_element_type=F32)


def split(value):
    high = value.astype(BF16)
    return high, (value - high.astype(F32)).astype(BF16)


def regroup(values):
    lane = iota((ROWS, 128), 1)
    for bit in range(4):
        low = 1 << bit
        width = ROWS * low
        keep = (lane & width) == 0
        moved = list(values)
        for first in range(PAIRS):
            if first & low:
                continue
            second = first | low
            moved[first] = jnp.where(keep, values[first], pltpu.roll(values[second], width, 1))
            moved[second] = jnp.where(keep, pltpu.roll(values[first], 128 - width, 1), values[second])
        values = moved
    return values


def kernel(
    strain, inv_asd, spectra, cutoff, high_table, low_table, series, peak,
    table, table_low, strain_v, asd_v, spectra_v, cut_s, gathered, partial, partials,
    weights, outgoing, received, bests,
    load_sem, z_send, z_recv, w_send, w_recv, done_sem, ready_sem, f_send, f_recv, t_send, t_recv,
):
    me_t = lax.axis_index("tmpl")
    me_f = lax.axis_index("freq")
    z_pos = me_f // NW
    w_pos = me_f % NW
    core = me_f % NC
    x_pos = me_t // NH
    half = me_t % NH
    y_full = half * NY + w_pos // NC

    loads = [
        pltpu.make_async_copy(strain, strain_v, load_sem.at[0]),
        pltpu.make_async_copy(spectra.at[:, :, :, pl.ds(0, BAND)], spectra_v, load_sem.at[1]),
        pltpu.make_async_copy(inv_asd.at[:, pl.ds(0, BAND)], asd_v, load_sem.at[2]),
        pltpu.make_async_copy(cutoff, cut_s, load_sem.at[3]),
        pltpu.make_async_copy(high_table, table, load_sem.at[4]),
        pltpu.make_async_copy(low_table, table_low, load_sem.at[5]),
    ]
    for load in loads:
        load.start()

    barrier = pltpu.get_barrier_semaphore()

    def greet(device):
        pl.semaphore_signal(barrier, inc=1, device_id=device, device_id_type=MESH)

    for step in FAR_FIRST:
        greet((me_t, (z_pos + step) % NZ * NW + w_pos))
    for away in (3, 5, 2, 6, 1, 7):
        place = (y_full + away) % (NH * NY)
        for to_core in range(NC):
            greet((x_pos * NH + place // NY, z_pos * NW + place % NY * NC + to_core))
    greet((me_t, me_f + 1 - 2 * core))
    for step in (2, 1, 3):
        greet(((x_pos + step) % NX * NH + half, me_f))

    loads[0].wait()
    own = strain_v[...]
    gathered[z_pos] = jnp.concatenate([own[:, :BAND], own[:, BAND:]], 0).astype(BF16)

    pl.semaphore_wait(barrier, NZ - 1 + (NH * NY - 2) * NC + 1 + NX - 1)

    for step in FAR_FIRST:
        copy = pltpu.make_async_remote_copy(
            src_ref=gathered.at[z_pos], dst_ref=gathered.at[z_pos], send_sem=z_send, recv_sem=z_recv,
            device_id=(me_t, (z_pos + step) % NZ * NW + w_pos), device_id_type=MESH,
        )
        copy.start()

    row = iota((128, 128), 0)
    col = iota((128, 128), 1)
    freq_row = 64 * z_pos + 8 * (row // 16) + row % 8
    sample_row = 64 * (col // 16) + 8 * w_pos + col % 8
    turns = (freq_row * sample_row + 128 * (row // 8 % 2)) & (SIDE - 1)
    first = jnp.cos(turns.astype(F32) * (2.0 * math.pi / SIDE))
    side = col // 8 % 2
    first = jnp.concatenate([jnp.where(side == 0, first, 0.0), jnp.where(side == 1, first, 0.0)], 0)
    first_high, first_low = split(first)
    twist = (ROWS * me_f + iota((ROWS, SIDE), 0)) * iota((ROWS, SIDE), 1)
    twist = twist.astype(F32) * (2.0 * math.pi / TOTAL)
    twist_cos = jnp.cos(twist)
    twist_sin = jnp.sin(twist)

    loads[1].wait()
    loads[2].wait()
    loads[3].wait()
    wanted = row % 8 * PAIRS + row // 8 % 8 * 2 + row // 64
    order = jnp.where(col == wanted, 1.0, 0.0).astype(BF16)
    sorted_spectra = dot(order, spectra_v[...].reshape(128, BAND))
    scale = asd_v[...]
    lane = iota((ROWS, BAND), 1)
    for templ in range(TEMPL):
        gain = jnp.where(lane < cut_s[templ], scale, 0.0)
        for part in range(2):
            block = slice((part * TEMPL + templ) * ROWS, (part * TEMPL + templ + 1) * ROWS)
            weights[block, :] = sorted_spectra[block, :] * gain

    pltpu.make_async_copy(gathered.at[pl.ds(0, NZ - 1)], gathered.at[pl.ds(0, NZ - 1)], z_recv).wait()
    for step in range(1, NW):
        pl.semaphore_signal(
            done_sem, inc=1, device_id=(me_t, z_pos * NW + (w_pos + step) % NW), device_id_type=MESH
        )
    blocks = gathered[...].reshape(128, BAND)
    shares = dot(first_high, blocks) + dot(first_low, blocks)
    partial[:, :, :BAND] = shares[:128].reshape(NW, 16, BAND).astype(BF16)
    partial[:, :, BAND:] = shares[128:].reshape(NW, 16, BAND).astype(BF16)
    for step in range(NY):
        for to_core in range(NC):
            if step == 2:
                away = 2 if to_core == 0 else 6
            else:
                away = (0, 1, 2, 7)[step]
            place = (y_full + away) % (NH * NY)
            target_core = to_core
            target_w = place % NY * NC + target_core
            if step == 0:
                if to_core == 0:
                    continue
                target_w = w_pos // NC * NC + (1 - core)
            copy = pltpu.make_async_remote_copy(
                src_ref=partial.at[target_w], dst_ref=partials.at[w_pos], send_sem=w_send, recv_sem=w_recv,
                device_id=(x_pos * NH + place // NY, z_pos * NW + target_w), device_id_type=MESH,
            )
            copy.start()
    partials[w_pos] = partial[w_pos]
    pltpu.make_async_copy(partials.at[pl.ds(0, NW - 1)], partials.at[pl.ds(0, NW - 1)], w_recv).wait()
    for step in range(1, NX):
        pl.semaphore_signal(
            ready_sem, inc=1, device_id=((x_pos + step) % NX * NH + half, me_f), device_id_type=MESH
        )
    sums = partials[0].astype(F32)
    for slot in range(1, NW):
        sums = sums + partials[slot].astype(F32)
    sum_real = sums[:ROWS]
    sum_imag = sums[ROWS:]
    turned = jnp.concatenate(
        [sum_real * twist_cos + sum_imag * twist_sin, sum_imag * twist_cos - sum_real * twist_sin], 0
    )
    turned_high, turned_low = split(turned)

    loads[4].wait()
    loads[5].wait()
    both = jnp.concatenate([turned_high, turned_low], 0)
    by_cos = dot(both, table[:, :BAND])
    by_sin = dot(both, table[:, SIDE : SIDE + BAND])
    by_cos = by_cos[:16] + by_cos[16:] + dot(turned_high, table_low[:, :BAND])
    by_sin = by_sin[:16] + by_sin[16:] + dot(turned_high, table_low[:, BAND:])
    spec_real = by_cos[:ROWS] + by_sin[ROWS:]
    spec_imag = by_cos[ROWS:] - by_sin[:ROWS]

    product = []
    for templ in range(TEMPL):
        gain_real = weights[templ * ROWS : (templ + 1) * ROWS, :]
        gain_imag = weights[(TEMPL + templ) * ROWS : (TEMPL + templ + 1) * ROWS, :]
        product.append(spec_real * gain_real + spec_imag * gain_imag)
    for templ in range(TEMPL):
        gain_real = weights[templ * ROWS : (templ + 1) * ROWS, :]
        gain_imag = weights[(TEMPL + templ) * ROWS : (TEMPL + templ + 1) * ROWS, :]
        product.append(spec_imag * gain_real - spec_real * gain_imag)
    product = jnp.concatenate(product, 0).astype(BF16)

    pl.semaphore_wait(done_sem, NW - 1)
    for pair in range(2):
        start = pair * 256
        by_cos = dot(product, table[:BAND, start : start + 256])
        by_sin = dot(product, table[:BAND, SIDE + start : SIDE + start + 256])
        for inner in range(2):
            column = 2 * pair + inner
            here = slice(inner * 128, (inner + 1) * 128)
            cos_here = twist_cos[:, column * 128 : (column + 1) * 128]
            sin_here = twist_sin[:, column * 128 : (column + 1) * 128]
            reals = []
            imags = []
            for templ in range(TEMPL):
                up = slice(templ * ROWS, (templ + 1) * ROWS)
                down = slice((TEMPL + templ) * ROWS, (TEMPL + templ + 1) * ROWS)
                real_part = by_cos[up, here] - by_sin[down, here]
                imag_part = by_sin[up, here] + by_cos[down, here]
                reals.append(real_part * cos_here - imag_part * sin_here)
                imags.append(real_part * sin_here + imag_part * cos_here)
            for slot, tile in enumerate(regroup(reals + imags)):
                outgoing[column * 16 + slot] = tile.astype(BF16)

    for target_z in (0, 1, 2, 3, 7, 4, 6, 5):
        def send(step, carry, target_z=target_z):
            target = target_z * NW + (w_pos + step) % NW

            @pl.when(target != me_f)
            def _():
                pltpu.make_async_remote_copy(
                    src_ref=outgoing.at[target], dst_ref=received.at[me_f], send_sem=f_send, recv_sem=f_recv,
                    device_id=(me_t, target), device_id_type=MESH,
                ).start()

            return carry

        lax.fori_loop(0, NW, send, 0)
    received[me_f] = outgoing[me_f]
    pltpu.make_async_copy(received.at[pl.ds(0, NF - 1)], received.at[pl.ds(0, NF - 1)], f_recv).wait()

    columns_in = jnp.transpose(received[...].reshape(SIDE, 128))
    for pair in range(2):
        start = pair * 256
        by_cos = dot(columns_in, table[:, start : start + 256]) * (1.0 / TOTAL)
        by_sin = dot(columns_in, table[:, SIDE + start : SIDE + start + 256]) * (1.0 / TOTAL)
        top = None
        for templ in range(TEMPL):
            up = slice(templ * ROWS, (templ + 1) * ROWS)
            down = slice((TEMPL + templ) * ROWS, (TEMPL + templ + 1) * ROWS)
            real_part = by_cos[up] - by_sin[down]
            imag_part = by_sin[up] + by_cos[down]
            series[templ, 0, :, start : start + 256] = real_part
            series[templ, 1, :, start : start + 256] = imag_part
            power = real_part * real_part + imag_part * imag_part
            top = power if top is None else jnp.maximum(top, power)
        bests[me_t, :, start : start + 256] = top.astype(BF16)

    pl.semaphore_wait(ready_sem, NX - 1)
    for away in ((2, 1), (1, 1), (3, 1), (0, 1), (2, 0), (1, 0), (3, 0)):
        pltpu.make_async_remote_copy(
            src_ref=bests.at[me_t], dst_ref=bests.at[me_t], send_sem=t_send, recv_sem=t_recv,
            device_id=((x_pos + away[0]) % NX * NH + (half + away[1]) % NH, me_f), device_id_type=MESH,
        ).start()
    others = NX * NH - 1
    pltpu.make_async_copy(bests.at[pl.ds(0, others)], bests.at[pl.ds(0, others)], t_recv).wait()
    tops = [bests[slot].astype(F32) for slot in range(NX * NH)]
    while len(tops) > 1:
        tops = [jnp.maximum(tops[i], tops[i + 1]) for i in range(0, len(tops), 2)]
    peak[...] = tops[0]

    pltpu.make_async_copy(gathered.at[pl.ds(0, NZ - 1)], gathered.at[pl.ds(0, NZ - 1)], z_send).wait()
    pltpu.make_async_copy(partial.at[pl.ds(0, NW - 1)], partial.at[pl.ds(0, NW - 1)], w_send).wait()
    pltpu.make_async_copy(outgoing.at[pl.ds(0, NF - 1)], outgoing.at[pl.ds(0, NF - 1)], f_send).wait()
    pltpu.make_async_copy(bests.at[pl.ds(0, others)], bests.at[pl.ds(0, others)], t_send).wait()


def store(series_v, peak_v, series, peak, sems):
    copies = [
        pltpu.make_async_copy(series_v, series, sems.at[0]),
        pltpu.make_async_copy(peak_v, peak, sems.at[1]),
    ]
    for copy in copies:
        copy.start()
    for copy in copies:
        copy.wait()


def local(strain, inv_asd, spectra, cutoff):
    high, low = base_tables()
    anywhere = pl.BlockSpec(memory_space=pl.ANY)
    inside = pl.BlockSpec(memory_space=pltpu.VMEM)
    dma = pltpu.SemaphoreType.DMA
    series, peak = pl.pallas_call(
        kernel,
        out_shape=(
            pltpu.VMEM((TEMPL, 2, ROWS, SIDE), F32),
            pltpu.VMEM((ROWS, SIDE), F32),
        ),
        in_specs=[anywhere] * 6,
        out_specs=(inside, inside),
        scratch_shapes=[
            pltpu.VMEM((SIDE, 2 * SIDE), BF16),
            pltpu.VMEM((SIDE, SIDE), BF16),
            pltpu.VMEM((ROWS, SIDE), F32),
            pltpu.VMEM((ROWS, BAND), F32),
            pltpu.VMEM((ROWS, TEMPL, 2, BAND), BF16),
            pltpu.SMEM((TEMPL,), jnp.int32),
            pltpu.VMEM((NZ, 16, BAND), BF16),
            pltpu.VMEM((NW, 16, SIDE), BF16),
            pltpu.VMEM((NW, 16, SIDE), BF16),
            pltpu.VMEM((128, BAND), F32),
            pltpu.VMEM((NF, ROWS, 128), BF16),
            pltpu.VMEM((NF, ROWS, 128), BF16),
            pltpu.VMEM((NX * NH, ROWS, SIDE), BF16),
            dma((6,)), dma, dma, dma, dma, pltpu.SemaphoreType.REGULAR, pltpu.SemaphoreType.REGULAR,
            dma, dma, dma, dma,
        ],
        compiler_params=pltpu.CompilerParams(collective_id=0, has_side_effects=True),
    )(strain, inv_asd, spectra, cutoff, jnp.asarray(high), jnp.asarray(low))
    return pl.pallas_call(
        store,
        out_shape=(
            jax.ShapeDtypeStruct((TEMPL, 2, ROWS, SIDE), F32),
            jax.ShapeDtypeStruct((ROWS, SIDE), F32),
        ),
        in_specs=[anywhere, anywhere],
        out_specs=(anywhere, anywhere),
        scratch_shapes=[dma((2,))],
    )(pltpu.with_memory_space_constraint(series, pltpu.VMEM), pltpu.with_memory_space_constraint(peak, pltpu.VMEM))


def solution(mesh):
    in_specs = (P("freq", None), P("freq", None), P("freq", "tmpl", None, None), P("tmpl"))
    out_specs = (P("tmpl", None, "freq", None), P("freq", None))
    return jax.shard_map(local, mesh=mesh, in_specs=in_specs, out_specs=out_specs, check_vma=False)
```

```python
import functools
import math

import jax
import jax.numpy as jnp
import numpy as np
from jax import lax
from jax.experimental import pallas as pl
from jax.experimental.pallas import tpu as pltpu
from jax.sharding import PartitionSpec as P

SIDE = 512
BAND = 256
TOTAL = SIDE * SIDE
NZ = 8
NY = 4
NC = 2
NW = NY * NC
NX = 4
NH = 2
NF = NZ * NW
ROWS = SIDE // NF
TEMPL = 8
PAIRS = 2 * TEMPL
EARLY = NZ // 2
MESH = pl.DeviceIdType.MESH
F32 = jnp.float32
BF16 = jnp.bfloat16


def base_tables():
    index = np.arange(SIDE)
    angle = 2.0 * np.pi / SIDE * (np.outer(index, index) % SIDE)
    cosines = np.cos(angle).astype(np.float32)
    sines = np.sin(angle).astype(np.float32)
    whole = np.concatenate([cosines, sines], 1)
    high = whole.astype(jnp.bfloat16)
    part = np.concatenate([cosines[:, :BAND], sines[:, :BAND]], 1)
    low = (part - part.astype(jnp.bfloat16).astype(np.float32)).astype(jnp.bfloat16)
    return high, low


def iota(shape, axis):
    return lax.broadcasted_iota(jnp.int32, shape, axis)


def dot(left, right):
    return jnp.dot(left, right, preferred_element_type=F32)


def split(value):
    high = value.astype(BF16)
    return high, (value - high.astype(F32)).astype(BF16)


def regroup(values):
    lane = iota((ROWS, 128), 1)
    for bit in range(4):
        low = 1 << bit
        width = ROWS * low
        keep = (lane & width) == 0
        moved = list(values)
        for first in range(PAIRS):
            if first & low:
                continue
            second = first | low
            moved[first] = jnp.where(keep, values[first], pltpu.roll(values[second], width, 1))
            moved[second] = jnp.where(keep, pltpu.roll(values[first], 128 - width, 1), values[second])
        values = moved
    return values


def kernel(
    strain, inv_asd, spectra, cutoff, high_table, low_table, series, peak,
    table, table_low, strain_v, asd_v, spectra_v, cut_s, gathered, partial, partials,
    weights, outgoing, received, bests, mirror_out, mirror_in, early_out, early_in, early_sum, mirror_sum,
    load_sem, z_send, early_recv, late_recv, late_sem, o_send, o_recv, e_send, e_recv, m_send, m_recv, w_send, w_recv, done_sem, ready_sem, f_send, f_recv, t_send, t_recv,
):
    me_t = lax.axis_index("tmpl")
    me_f = lax.axis_index("freq")
    z_pos = me_f // NW
    w_pos = me_f % NW
    core = me_f % NC
    x_pos = me_t // NH
    half = me_t % NH
    y_full = half * NY + w_pos // NC

    loads = [
        pltpu.make_async_copy(strain, strain_v, load_sem.at[0]),
        pltpu.make_async_copy(spectra.at[:, :, :, pl.ds(0, BAND)], spectra_v, load_sem.at[1]),
        pltpu.make_async_copy(inv_asd.at[:, pl.ds(0, BAND)], asd_v, load_sem.at[2]),
        pltpu.make_async_copy(cutoff, cut_s, load_sem.at[3]),
        pltpu.make_async_copy(high_table, table, load_sem.at[4]),
        pltpu.make_async_copy(low_table, table_low, load_sem.at[5]),
    ]
    for load in loads:
        load.start()

    barrier = pltpu.get_barrier_semaphore()

    def greet(device):
        pl.semaphore_signal(barrier, inc=1, device_id=device, device_id_type=MESH)

    early = z_pos < EARLY
    late = jnp.logical_not(early)
    mirror = NZ - 1 - z_pos
    base_z = z_pos // EARLY * EARLY
    for step in (3, 1, 2):
        greet((me_t, (base_z + (z_pos + step) % EARLY) * NW + w_pos))

    @pl.when(early)
    def _():
        for late_z in range(EARLY, NZ):
            greet((me_t, late_z * NW + w_pos))

    for away in (3, 5, 2, 6, 1, 7):
        place = (y_full + away) % (NH * NY)
        for to_core in range(NC):
            greet((x_pos * NH + place // NY, z_pos * NW + place % NY * NC + to_core))
    greet((me_t, me_f + 1 - 2 * core))
    for step in (2, 1, 3):
        greet(((x_pos + step) % NX * NH + half, me_f))

    loads[0].wait()
    own = strain_v[...]
    gathered[z_pos] = jnp.concatenate([own[:, :BAND], own[:, BAND:]], 0).astype(BF16)

    alike = EARLY - 1 + (NH * NY - 2) * NC + 1 + NX - 1

    def give(to_z, recv_sem):
        pltpu.make_async_remote_copy(
            src_ref=gathered.at[z_pos], dst_ref=gathered.at[z_pos], send_sem=z_send, recv_sem=recv_sem,
            device_id=(me_t, to_z * NW + w_pos), device_id_type=MESH,
        ).start()

    def arrived(count, sem):
        pltpu.make_async_copy(gathered.at[pl.ds(0, count)], gathered.at[pl.ds(0, count)], sem).wait()

    def tell_line():
        for step in range(1, NW):
            pl.semaphore_signal(
                done_sem, inc=1, device_id=(me_t, z_pos * NW + (w_pos + step) % NW), device_id_type=MESH
            )

    def first_table(z_rows, z_first):
        row = iota((128, 64), 0)
        col = iota((128, 64), 1)
        freq_row = 64 * z_rows + 8 * (row // 16) + row % 8
        sample_row = 64 * (z_first + col // 16) + 8 * w_pos + col % 8
        turns = (freq_row * sample_row + 128 * (row // 8 % 2)) & (SIDE - 1)
        values = jnp.cos(turns.astype(F32) * (2.0 * math.pi / SIDE))
        side = col // 8 % 2
        return jnp.concatenate([jnp.where(side == 0, values, 0.0), jnp.where(side == 1, values, 0.0)], 0)

    def to_group(source, target, send_sem, recv_sem):
        for step, to_core in ((2, 0), (2, 1), (1, 0), (1, 1), (3, 0), (3, 1), (0, 1)):
            if step == 2:
                place = (y_full + (2 if to_core == 0 else 6)) % (NH * NY)
            else:
                place = (y_full + (0, 1, 0, 7)[step]) % (NH * NY)
            target_w = place % NY * NC + (1 - core if step == 0 else to_core)
            pltpu.make_async_remote_copy(
                src_ref=source.at[target_w], dst_ref=target.at[w_pos], send_sem=send_sem, recv_sem=recv_sem,
                device_id=(x_pos * NH + place // NY, z_pos * NW + target_w), device_id_type=MESH,
            ).start()
        target[w_pos] = source[w_pos]

    def first_share(tables, first_z, out):
        blocks = gathered[first_z : first_z + EARLY].reshape(64, BAND)
        shares = dot(tables[0], blocks) + dot(tables[1], blocks)
        out[:, :, :BAND] = shares[:128].reshape(NW, 16, BAND).astype(BF16)
        out[:, :, BAND:] = shares[128:].reshape(NW, 16, BAND).astype(BF16)

    def total(ref):
        sums = ref[0].astype(F32)
        for slot in range(1, NW):
            sums = sums + ref[slot].astype(F32)
        return sums

    def came(ref, sem):
        pltpu.make_async_copy(ref.at[pl.ds(0, NW - 1)], ref.at[pl.ds(0, NW - 1)], sem).wait()

    @pl.when(late)
    def _():
        pl.semaphore_wait(barrier, alike + EARLY)
        for step in (3, 1, 2):
            give(EARLY + (z_pos + step) % EARLY, late_recv)
        for to_z in range(EARLY):
            give(to_z, late_recv)
        pl.semaphore_signal(late_sem, inc=1, device_id=(me_t, mirror * NW + w_pos), device_id_type=MESH)
        tell_line()

    @pl.when(early)
    def _():
        pl.semaphore_wait(barrier, alike)
        for step in (3, 1, 2):
            give((z_pos + step) % EARLY, early_recv)
        mirror_tables = split(first_table(mirror, 0))
        own_tables = split(first_table(z_pos, 0))
        arrived(EARLY - 1, early_recv)
        first_share(mirror_tables, 0, mirror_out)
        to_group(mirror_out, mirror_in, o_send, o_recv)
        first_share(own_tables, 0, early_out)
        to_group(early_out, early_in, e_send, e_recv)

    row = iota((128, 128), 0)
    col = iota((128, 128), 1)
    late_tables = split(first_table(z_pos, EARLY))
    twist = (ROWS * me_f + iota((ROWS, SIDE), 0)) * iota((ROWS, SIDE), 1)
    twist = twist.astype(F32) * (2.0 * math.pi / TOTAL)
    twist_cos = jnp.cos(twist)
    twist_sin = jnp.sin(twist)

    loads[1].wait()
    loads[2].wait()
    loads[3].wait()
    wanted = row % 8 * PAIRS + row // 8 % 8 * 2 + row // 64
    order = jnp.where(col == wanted, 1.0, 0.0).astype(BF16)
    sorted_spectra = dot(order, spectra_v[...].reshape(128, BAND))
    scale = asd_v[...]
    lane = iota((ROWS, BAND), 1)
    for templ in range(TEMPL):
        gain = jnp.where(lane < cut_s[templ], scale, 0.0)
        for part in range(2):
            block = slice((part * TEMPL + templ) * ROWS, (part * TEMPL + templ + 1) * ROWS)
            weights[block, :] = sorted_spectra[block, :] * gain

    @pl.when(early)
    def _():
        came(mirror_in, o_recv)
        mirror_sum[...] = total(mirror_in)
        pl.semaphore_wait(late_sem, 1)
        pltpu.make_async_remote_copy(
            src_ref=mirror_sum, dst_ref=early_sum, send_sem=m_send, recv_sem=m_recv,
            device_id=(me_t, mirror * NW + w_pos), device_id_type=MESH,
        ).start()
        arrived(EARLY, late_recv)

    @pl.when(late)
    def _():
        arrived(EARLY - 1, late_recv)

    first_share(late_tables, EARLY, partial)
    to_group(partial, partials, w_send, w_recv)

    @pl.when(early)
    def _():
        tell_line()
        came(early_in, e_recv)
        early_sum[...] = total(early_in)

    @pl.when(late)
    def _():
        pltpu.make_async_copy(mirror_sum, early_sum, m_recv).wait()

    came(partials, w_recv)
    for step in range(1, NX):
        pl.semaphore_signal(
            ready_sem, inc=1, device_id=((x_pos + step) % NX * NH + half, me_f), device_id_type=MESH
        )
    sums = early_sum[...] + total(partials)
    sum_real = sums[:ROWS]
    sum_imag = sums[ROWS:]
    turned = jnp.concatenate(
        [sum_real * twist_cos + sum_imag * twist_sin, sum_imag * twist_cos - sum_real * twist_sin], 0
    )
    turned_high, turned_low = split(turned)

    loads[4].wait()
    loads[5].wait()
    both = jnp.concatenate([turned_high, turned_low], 0)
    by_cos = dot(both, table[:, :BAND])
    by_sin = dot(both, table[:, SIDE : SIDE + BAND])
    by_cos = by_cos[:16] + by_cos[16:] + dot(turned_high, table_low[:, :BAND])
    by_sin = by_sin[:16] + by_sin[16:] + dot(turned_high, table_low[:, BAND:])
    spec_real = by_cos[:ROWS] + by_sin[ROWS:]
    spec_imag = by_cos[ROWS:] - by_sin[:ROWS]

    product = []
    for templ in range(TEMPL):
        gain_real = weights[templ * ROWS : (templ + 1) * ROWS, :]
        gain_imag = weights[(TEMPL + templ) * ROWS : (TEMPL + templ + 1) * ROWS, :]
        product.append(spec_real * gain_real + spec_imag * gain_imag)
    for templ in range(TEMPL):
        gain_real = weights[templ * ROWS : (templ + 1) * ROWS, :]
        gain_imag = weights[(TEMPL + templ) * ROWS : (TEMPL + templ + 1) * ROWS, :]
        product.append(spec_imag * gain_real - spec_real * gain_imag)
    product = jnp.concatenate(product, 0).astype(BF16)

    pl.semaphore_wait(done_sem, NW - 1)
    for pair in range(2):
        start = pair * 256
        by_cos = dot(product, table[:BAND, start : start + 256])
        by_sin = dot(product, table[:BAND, SIDE + start : SIDE + start + 256])
        for inner in range(2):
            column = 2 * pair + inner
            here = slice(inner * 128, (inner + 1) * 128)
            cos_here = twist_cos[:, column * 128 : (column + 1) * 128]
            sin_here = twist_sin[:, column * 128 : (column + 1) * 128]
            reals = []
            imags = []
            for templ in range(TEMPL):
                up = slice(templ * ROWS, (templ + 1) * ROWS)
                down = slice((TEMPL + templ) * ROWS, (TEMPL + templ + 1) * ROWS)
                real_part = by_cos[up, here] - by_sin[down, here]
                imag_part = by_sin[up, here] + by_cos[down, here]
                reals.append(real_part * cos_here - imag_part * sin_here)
                imags.append(real_part * sin_here + imag_part * cos_here)
            for slot, tile in enumerate(regroup(reals + imags)):
                outgoing[column * 16 + slot] = tile.astype(BF16)

    for target_z in (0, 1, 2, 3, 7, 4, 6, 5):
        def send(step, carry, target_z=target_z):
            target = target_z * NW + (w_pos + step) % NW

            @pl.when(target != me_f)
            def _():
                pltpu.make_async_remote_copy(
                    src_ref=outgoing.at[target], dst_ref=received.at[me_f], send_sem=f_send, recv_sem=f_recv,
                    device_id=(me_t, target), device_id_type=MESH,
                ).start()

            return carry

        lax.fori_loop(0, NW, send, 0)
    received[me_f] = outgoing[me_f]
    pltpu.make_async_copy(received.at[pl.ds(0, NF - 1)], received.at[pl.ds(0, NF - 1)], f_recv).wait()

    columns_in = jnp.transpose(received[...].reshape(SIDE, 128))
    for pair in range(2):
        start = pair * 256
        by_cos = dot(columns_in, table[:, start : start + 256]) * (1.0 / TOTAL)
        by_sin = dot(columns_in, table[:, SIDE + start : SIDE + start + 256]) * (1.0 / TOTAL)
        top = None
        for templ in range(TEMPL):
            up = slice(templ * ROWS, (templ + 1) * ROWS)
            down = slice((TEMPL + templ) * ROWS, (TEMPL + templ + 1) * ROWS)
            real_part = by_cos[up] - by_sin[down]
            imag_part = by_sin[up] + by_cos[down]
            series[templ, 0, :, start : start + 256] = real_part
            series[templ, 1, :, start : start + 256] = imag_part
            power = real_part * real_part + imag_part * imag_part
            top = power if top is None else jnp.maximum(top, power)
        bests[me_t, :, start : start + 256] = top.astype(BF16)

    pl.semaphore_wait(ready_sem, NX - 1)
    for away in ((2, 1), (1, 1), (3, 1), (0, 1), (2, 0), (1, 0), (3, 0)):
        pltpu.make_async_remote_copy(
            src_ref=bests.at[me_t], dst_ref=bests.at[me_t], send_sem=t_send, recv_sem=t_recv,
            device_id=((x_pos + away[0]) % NX * NH + (half + away[1]) % NH, me_f), device_id_type=MESH,
        ).start()
    others = NX * NH - 1
    pltpu.make_async_copy(bests.at[pl.ds(0, others)], bests.at[pl.ds(0, others)], t_recv).wait()
    tops = [bests[slot].astype(F32) for slot in range(NX * NH)]
    while len(tops) > 1:
        tops = [jnp.maximum(tops[i], tops[i + 1]) for i in range(0, len(tops), 2)]
    peak[...] = tops[0]

    @pl.when(early)
    def _():
        arrived(EARLY - 1, z_send)
        came(mirror_out, o_send)
        came(early_out, e_send)
        pltpu.make_async_copy(mirror_sum, early_sum, m_send).wait()

    @pl.when(late)
    def _():
        arrived(NZ - 1, z_send)

    came(partial, w_send)
    pltpu.make_async_copy(outgoing.at[pl.ds(0, NF - 1)], outgoing.at[pl.ds(0, NF - 1)], f_send).wait()
    pltpu.make_async_copy(bests.at[pl.ds(0, others)], bests.at[pl.ds(0, others)], t_send).wait()


def store(series_v, peak_v, series, peak, sems):
    copies = [
        pltpu.make_async_copy(series_v, series, sems.at[0]),
        pltpu.make_async_copy(peak_v, peak, sems.at[1]),
    ]
    for copy in copies:
        copy.start()
    for copy in copies:
        copy.wait()


def local(strain, inv_asd, spectra, cutoff):
    high, low = base_tables()
    anywhere = pl.BlockSpec(memory_space=pl.ANY)
    inside = pl.BlockSpec(memory_space=pltpu.VMEM)
    dma = pltpu.SemaphoreType.DMA
    series, peak = pl.pallas_call(
        kernel,
        out_shape=(
            pltpu.VMEM((TEMPL, 2, ROWS, SIDE), F32),
            pltpu.VMEM((ROWS, SIDE), F32),
        ),
        in_specs=[anywhere] * 6,
        out_specs=(inside, inside),
        scratch_shapes=[
            pltpu.VMEM((SIDE, 2 * SIDE), BF16),
            pltpu.VMEM((SIDE, SIDE), BF16),
            pltpu.VMEM((ROWS, SIDE), F32),
            pltpu.VMEM((ROWS, BAND), F32),
            pltpu.VMEM((ROWS, TEMPL, 2, BAND), BF16),
            pltpu.SMEM((TEMPL,), jnp.int32),
            pltpu.VMEM((NZ, 16, BAND), BF16),
            pltpu.VMEM((NW, 16, SIDE), BF16),
            pltpu.VMEM((NW, 16, SIDE), BF16),
            pltpu.VMEM((128, BAND), F32),
            pltpu.VMEM((NF, ROWS, 128), BF16),
            pltpu.VMEM((NF, ROWS, 128), BF16),
            pltpu.VMEM((NX * NH, ROWS, SIDE), BF16),
            pltpu.VMEM((NW, 16, SIDE), BF16),
            pltpu.VMEM((NW, 16, SIDE), BF16),
            pltpu.VMEM((NW, 16, SIDE), BF16),
            pltpu.VMEM((NW, 16, SIDE), BF16),
            pltpu.VMEM((16, SIDE), F32),
            pltpu.VMEM((16, SIDE), F32),
            dma((6,)), dma, dma, dma, pltpu.SemaphoreType.REGULAR, dma, dma, dma, dma, dma, dma, dma, dma,
            pltpu.SemaphoreType.REGULAR, pltpu.SemaphoreType.REGULAR,
            dma, dma, dma, dma,
        ],
        compiler_params=pltpu.CompilerParams(collective_id=0, has_side_effects=True),
    )(strain, inv_asd, spectra, cutoff, jnp.asarray(high), jnp.asarray(low))
    return pl.pallas_call(
        store,
        out_shape=(
            jax.ShapeDtypeStruct((TEMPL, 2, ROWS, SIDE), F32),
            jax.ShapeDtypeStruct((ROWS, SIDE), F32),
        ),
        in_specs=[anywhere, anywhere],
        out_specs=(anywhere, anywhere),
        scratch_shapes=[dma((2,))],
    )(pltpu.with_memory_space_constraint(series, pltpu.VMEM), pltpu.with_memory_space_constraint(peak, pltpu.VMEM))


def solution(mesh):
    in_specs = (P("freq", None), P("freq", None), P("freq", "tmpl", None, None), P("tmpl"))
    out_specs = (P("tmpl", None, "freq", None), P("freq", None))
    return jax.shard_map(local, mesh=mesh, in_specs=in_specs, out_specs=out_specs, check_vma=False)
```

```python
import functools
import math

import jax
import jax.numpy as jnp
import numpy as np
from jax import lax
from jax.experimental import pallas as pl
from jax.experimental.pallas import tpu as pltpu
from jax.sharding import PartitionSpec as P

SIDE = 512
BAND = 256
TOTAL = SIDE * SIDE
NZ = 8
NY = 4
NC = 2
NW = NY * NC
NX = 4
NH = 2
NF = NZ * NW
ROWS = SIDE // NF
TEMPL = 8
PAIRS = 2 * TEMPL
EARLY = NZ // 2
MESH = pl.DeviceIdType.MESH
F32 = jnp.float32
BF16 = jnp.bfloat16


def base_tables():
    index = np.arange(SIDE)
    angle = 2.0 * np.pi / SIDE * (np.outer(index, index) % SIDE)
    cosines = np.cos(angle).astype(np.float32)
    sines = np.sin(angle).astype(np.float32)
    whole = np.concatenate([cosines, sines], 1)
    high = whole.astype(jnp.bfloat16)
    part = np.concatenate([cosines[:, :BAND], sines[:, :BAND]], 1)
    low = (part - part.astype(jnp.bfloat16).astype(np.float32)).astype(jnp.bfloat16)
    return high, low


def iota(shape, axis):
    return lax.broadcasted_iota(jnp.int32, shape, axis)


def dot(left, right):
    return jnp.dot(left, right, preferred_element_type=F32)


def split(value):
    high = value.astype(BF16)
    return high, (value - high.astype(F32)).astype(BF16)


def regroup(values):
    lane = iota((ROWS, 128), 1)
    for bit in range(4):
        low = 1 << bit
        width = ROWS * low
        keep = (lane & width) == 0
        moved = list(values)
        for first in range(PAIRS):
            if first & low:
                continue
            second = first | low
            moved[first] = jnp.where(keep, values[first], pltpu.roll(values[second], width, 1))
            moved[second] = jnp.where(keep, pltpu.roll(values[first], 128 - width, 1), values[second])
        values = moved
    return values


def kernel(
    strain, inv_asd, spectra, cutoff, high_table, low_table, series, peak,
    table, table_low, strain_v, asd_v, spectra_v, cut_s, gathered, partial, partials,
    weights, outgoing, received, bests, mirror_out, mirror_in, early_out, early_in, early_sum, mirror_sum,
    load_sem, z_send, early_recv, late_recv, late_sem, o_send, o_recv, e_send, e_recv, m_send, m_recv, w_send, w_recv, done_sem, ready_sem, f_send, f_recv, t_send, t_recv,
):
    me_t = lax.axis_index("tmpl")
    me_f = lax.axis_index("freq")
    z_pos = me_f // NW
    w_pos = me_f % NW
    core = me_f % NC
    x_pos = me_t // NH
    half = me_t % NH
    y_full = half * NY + w_pos // NC

    loads = [
        pltpu.make_async_copy(strain, strain_v, load_sem.at[0]),
        pltpu.make_async_copy(spectra.at[:, :, :, pl.ds(0, BAND)], spectra_v, load_sem.at[1]),
        pltpu.make_async_copy(inv_asd.at[:, pl.ds(0, BAND)], asd_v, load_sem.at[2]),
        pltpu.make_async_copy(cutoff, cut_s, load_sem.at[3]),
        pltpu.make_async_copy(high_table, table, load_sem.at[4]),
        pltpu.make_async_copy(low_table, table_low, load_sem.at[5]),
    ]
    for load in loads:
        load.start()

    barrier = pltpu.get_barrier_semaphore()

    def greet(device):
        pl.semaphore_signal(barrier, inc=1, device_id=device, device_id_type=MESH)

    early = z_pos < EARLY
    late = jnp.logical_not(early)
    mirror = NZ - 1 - z_pos
    base_z = z_pos // EARLY * EARLY
    for step in (3, 1, 2):
        greet((me_t, (base_z + (z_pos + step) % EARLY) * NW + w_pos))

    @pl.when(early)
    def _():
        for late_z in range(EARLY, NZ):
            greet((me_t, late_z * NW + w_pos))

    for away in (3, 5, 2, 6, 1, 7):
        place = (y_full + away) % (NH * NY)
        for to_core in range(NC):
            greet((x_pos * NH + place // NY, z_pos * NW + place % NY * NC + to_core))
    greet((me_t, me_f + 1 - 2 * core))
    for step in (2, 1, 3):
        greet(((x_pos + step) % NX * NH + half, me_f))

    loads[0].wait()
    own = strain_v[...]
    gathered[z_pos] = jnp.concatenate([own[:, :BAND], own[:, BAND:]], 0).astype(BF16)

    alike = EARLY - 1 + (NH * NY - 2) * NC + 1 + NX - 1

    def give(to_z, recv_sem):
        pltpu.make_async_remote_copy(
            src_ref=gathered.at[z_pos], dst_ref=gathered.at[z_pos], send_sem=z_send, recv_sem=recv_sem,
            device_id=(me_t, to_z * NW + w_pos), device_id_type=MESH,
        ).start()

    def arrived(count, sem):
        pltpu.make_async_copy(gathered.at[pl.ds(0, count)], gathered.at[pl.ds(0, count)], sem).wait()

    def tell_line():
        for step in range(1, NW):
            pl.semaphore_signal(
                done_sem, inc=1, device_id=(me_t, z_pos * NW + (w_pos + step) % NW), device_id_type=MESH
            )

    def first_table(z_rows, z_first):
        row = iota((128, 64), 0)
        col = iota((128, 64), 1)
        freq_row = 64 * z_rows + 8 * (row // 16) + row % 8
        sample_row = 64 * (z_first + col // 16) + 8 * w_pos + col % 8
        turns = (freq_row * sample_row + 128 * (row // 8 % 2)) & (SIDE - 1)
        values = jnp.cos(turns.astype(F32) * (2.0 * math.pi / SIDE))
        side = col // 8 % 2
        return jnp.concatenate([jnp.where(side == 0, values, 0.0), jnp.where(side == 1, values, 0.0)], 0)

    def to_group(source, target, send_sem, recv_sem):
        for step, to_core in ((2, 0), (2, 1), (1, 0), (1, 1), (3, 0), (3, 1), (0, 1)):
            if step == 2:
                place = (y_full + (2 if to_core == 0 else 6)) % (NH * NY)
            else:
                place = (y_full + (0, 1, 0, 7)[step]) % (NH * NY)
            target_w = place % NY * NC + (1 - core if step == 0 else to_core)
            pltpu.make_async_remote_copy(
                src_ref=source.at[target_w], dst_ref=target.at[w_pos], send_sem=send_sem, recv_sem=recv_sem,
                device_id=(x_pos * NH + place // NY, z_pos * NW + target_w), device_id_type=MESH,
            ).start()
        target[w_pos] = source[w_pos]

    def first_share(tables, first_z, out):
        blocks = gathered[first_z : first_z + EARLY].reshape(64, BAND)
        shares = dot(tables[0], blocks) + dot(tables[1], blocks)
        out[:, :, :BAND] = shares[:128].reshape(NW, 16, BAND).astype(BF16)
        out[:, :, BAND:] = shares[128:].reshape(NW, 16, BAND).astype(BF16)

    def total(ref):
        sums = ref[0].astype(F32)
        for slot in range(1, NW):
            sums = sums + ref[slot].astype(F32)
        return sums

    def came(ref, sem):
        pltpu.make_async_copy(ref.at[pl.ds(0, NW - 1)], ref.at[pl.ds(0, NW - 1)], sem).wait()

    @pl.when(late)
    def _():
        pl.semaphore_wait(barrier, alike + EARLY)
        for step in (3, 1, 2):
            give(EARLY + (z_pos + step) % EARLY, late_recv)
        for to_z in range(EARLY):
            give(to_z, late_recv)
        pl.semaphore_signal(late_sem, inc=1, device_id=(me_t, mirror * NW + w_pos), device_id_type=MESH)
        tell_line()

    @pl.when(early)
    def _():
        pl.semaphore_wait(barrier, alike)
        for step in (3, 1, 2):
            give((z_pos + step) % EARLY, early_recv)
        mirror_tables = split(first_table(mirror, 0))
        own_tables = split(first_table(z_pos, 0))
        arrived(EARLY - 1, early_recv)
        first_share(mirror_tables, 0, mirror_out)
        to_group(mirror_out, mirror_in, o_send, o_recv)
        first_share(own_tables, 0, early_out)
        to_group(early_out, early_in, e_send, e_recv)

    row = iota((128, 128), 0)
    col = iota((128, 128), 1)
    late_tables = split(first_table(z_pos, EARLY))
    twist = (ROWS * me_f + iota((ROWS, SIDE), 0)) * iota((ROWS, SIDE), 1)
    twist = twist.astype(F32) * (2.0 * math.pi / TOTAL)
    twist_cos = jnp.cos(twist)
    twist_sin = jnp.sin(twist)

    loads[1].wait()
    loads[2].wait()
    loads[3].wait()
    wanted = row % 8 * PAIRS + row // 8 % 8 * 2 + row // 64
    order = jnp.where(col == wanted, 1.0, 0.0).astype(BF16)
    sorted_spectra = dot(order, spectra_v[...].reshape(128, BAND))
    scale = asd_v[...]
    lane = iota((ROWS, BAND), 1)
    for templ in range(TEMPL):
        gain = jnp.where(lane < cut_s[templ], scale, 0.0)
        for part in range(2):
            block = slice((part * TEMPL + templ) * ROWS, (part * TEMPL + templ + 1) * ROWS)
            weights[block, :] = sorted_spectra[block, :] * gain

    @pl.when(early)
    def _():
        came(mirror_in, o_recv)
        mirror_sum[...] = total(mirror_in)
        pl.semaphore_wait(late_sem, 1)
        pltpu.make_async_remote_copy(
            src_ref=mirror_sum, dst_ref=early_sum, send_sem=m_send, recv_sem=m_recv,
            device_id=(me_t, mirror * NW + w_pos), device_id_type=MESH,
        ).start()
        arrived(EARLY, late_recv)

    @pl.when(late)
    def _():
        arrived(EARLY - 1, late_recv)

    first_share(late_tables, EARLY, partial)
    to_group(partial, partials, w_send, w_recv)

    @pl.when(early)
    def _():
        tell_line()
        came(early_in, e_recv)
        early_sum[...] = total(early_in)

    @pl.when(late)
    def _():
        pltpu.make_async_copy(mirror_sum, early_sum, m_recv).wait()

    came(partials, w_recv)
    for step in range(1, NX):
        pl.semaphore_signal(
            ready_sem, inc=1, device_id=((x_pos + step) % NX * NH + half, me_f), device_id_type=MESH
        )
    sums = early_sum[...] + total(partials)
    sum_real = sums[:ROWS]
    sum_imag = sums[ROWS:]
    turned = jnp.concatenate(
        [sum_real * twist_cos + sum_imag * twist_sin, sum_imag * twist_cos - sum_real * twist_sin], 0
    )
    turned_high, turned_low = split(turned)

    loads[4].wait()
    loads[5].wait()
    both = jnp.concatenate([turned_high, turned_low], 0)
    by_cos = dot(both, table[:, :BAND])
    by_sin = dot(both, table[:, SIDE : SIDE + BAND])
    by_cos = by_cos[:16] + by_cos[16:] + dot(turned_high, table_low[:, :BAND])
    by_sin = by_sin[:16] + by_sin[16:] + dot(turned_high, table_low[:, BAND:])
    spec_real = by_cos[:ROWS] + by_sin[ROWS:]
    spec_imag = by_cos[ROWS:] - by_sin[:ROWS]

    product = []
    for templ in range(TEMPL):
        gain_real = weights[templ * ROWS : (templ + 1) * ROWS, :]
        gain_imag = weights[(TEMPL + templ) * ROWS : (TEMPL + templ + 1) * ROWS, :]
        product.append(spec_real * gain_real + spec_imag * gain_imag)
    for templ in range(TEMPL):
        gain_real = weights[templ * ROWS : (templ + 1) * ROWS, :]
        gain_imag = weights[(TEMPL + templ) * ROWS : (TEMPL + templ + 1) * ROWS, :]
        product.append(spec_imag * gain_real - spec_real * gain_imag)
    product = jnp.concatenate(product, 0).astype(BF16)

    def send(target):
        pltpu.make_async_remote_copy(
            src_ref=outgoing.at[target], dst_ref=received.at[me_f], send_sem=f_send, recv_sem=f_recv,
            device_id=(me_t, target), device_id_type=MESH,
        ).start()

    for column, target_zs in ((0, (0, 1)), (1, (2, 3)), (3, (7, 6)), (2, (4, 5))):
        start = column * 128
        by_cos = dot(product, table[:BAND, start : start + 128])
        by_sin = dot(product, table[:BAND, SIDE + start : SIDE + start + 128])
        cos_here = twist_cos[:, start : start + 128]
        sin_here = twist_sin[:, start : start + 128]
        reals = []
        imags = []
        for templ in range(TEMPL):
            up = slice(templ * ROWS, (templ + 1) * ROWS)
            down = slice((TEMPL + templ) * ROWS, (TEMPL + templ + 1) * ROWS)
            real_part = by_cos[up] - by_sin[down]
            imag_part = by_sin[up] + by_cos[down]
            reals.append(real_part * cos_here - imag_part * sin_here)
            imags.append(real_part * sin_here + imag_part * cos_here)
        for slot, tile in enumerate(regroup(reals + imags)):
            outgoing[column * 16 + slot] = tile.astype(BF16)
        if column == 0:
            pl.semaphore_wait(done_sem, NW - 1)
        for target_z in target_zs:

            def send_row(step, carry, target_z=target_z):
                target = target_z * NW + (w_pos + step) % NW
                pl.when(target != me_f)(functools.partial(send, target))
                return carry

            lax.fori_loop(0, NW, send_row, 0)

    received[me_f] = outgoing[me_f]
    pltpu.make_async_copy(received.at[pl.ds(0, NF - 1)], received.at[pl.ds(0, NF - 1)], f_recv).wait()

    columns_in = jnp.transpose(received[...].reshape(SIDE, 128))
    for pair in range(2):
        start = pair * 256
        by_cos = dot(columns_in, table[:, start : start + 256]) * (1.0 / TOTAL)
        by_sin = dot(columns_in, table[:, SIDE + start : SIDE + start + 256]) * (1.0 / TOTAL)
        top = None
        for templ in range(TEMPL):
            up = slice(templ * ROWS, (templ + 1) * ROWS)
            down = slice((TEMPL + templ) * ROWS, (TEMPL + templ + 1) * ROWS)
            real_part = by_cos[up] - by_sin[down]
            imag_part = by_sin[up] + by_cos[down]
            series[templ, 0, :, start : start + 256] = real_part
            series[templ, 1, :, start : start + 256] = imag_part
            power = real_part * real_part + imag_part * imag_part
            top = power if top is None else jnp.maximum(top, power)
        bests[me_t, :, start : start + 256] = top.astype(BF16)

    pl.semaphore_wait(ready_sem, NX - 1)
    for away in ((2, 1), (1, 1), (3, 1), (0, 1), (2, 0), (1, 0), (3, 0)):
        pltpu.make_async_remote_copy(
            src_ref=bests.at[me_t], dst_ref=bests.at[me_t], send_sem=t_send, recv_sem=t_recv,
            device_id=((x_pos + away[0]) % NX * NH + (half + away[1]) % NH, me_f), device_id_type=MESH,
        ).start()
    others = NX * NH - 1
    pltpu.make_async_copy(bests.at[pl.ds(0, others)], bests.at[pl.ds(0, others)], t_recv).wait()
    tops = [bests[slot].astype(F32) for slot in range(NX * NH)]
    while len(tops) > 1:
        tops = [jnp.maximum(tops[i], tops[i + 1]) for i in range(0, len(tops), 2)]
    peak[...] = tops[0]

    @pl.when(early)
    def _():
        arrived(EARLY - 1, z_send)
        came(mirror_out, o_send)
        came(early_out, e_send)
        pltpu.make_async_copy(mirror_sum, early_sum, m_send).wait()

    @pl.when(late)
    def _():
        arrived(NZ - 1, z_send)

    came(partial, w_send)
    pltpu.make_async_copy(outgoing.at[pl.ds(0, NF - 1)], outgoing.at[pl.ds(0, NF - 1)], f_send).wait()
    pltpu.make_async_copy(bests.at[pl.ds(0, others)], bests.at[pl.ds(0, others)], t_send).wait()


def store(series_v, peak_v, series, peak, sems):
    copies = [
        pltpu.make_async_copy(series_v, series, sems.at[0]),
        pltpu.make_async_copy(peak_v, peak, sems.at[1]),
    ]
    for copy in copies:
        copy.start()
    for copy in copies:
        copy.wait()


def local(strain, inv_asd, spectra, cutoff):
    high, low = base_tables()
    anywhere = pl.BlockSpec(memory_space=pl.ANY)
    inside = pl.BlockSpec(memory_space=pltpu.VMEM)
    dma = pltpu.SemaphoreType.DMA
    series, peak = pl.pallas_call(
        kernel,
        out_shape=(
            pltpu.VMEM((TEMPL, 2, ROWS, SIDE), F32),
            pltpu.VMEM((ROWS, SIDE), F32),
        ),
        in_specs=[anywhere] * 6,
        out_specs=(inside, inside),
        scratch_shapes=[
            pltpu.VMEM((SIDE, 2 * SIDE), BF16),
            pltpu.VMEM((SIDE, SIDE), BF16),
            pltpu.VMEM((ROWS, SIDE), F32),
            pltpu.VMEM((ROWS, BAND), F32),
            pltpu.VMEM((ROWS, TEMPL, 2, BAND), BF16),
            pltpu.SMEM((TEMPL,), jnp.int32),
            pltpu.VMEM((NZ, 16, BAND), BF16),
            pltpu.VMEM((NW, 16, SIDE), BF16),
            pltpu.VMEM((NW, 16, SIDE), BF16),
            pltpu.VMEM((128, BAND), F32),
            pltpu.VMEM((NF, ROWS, 128), BF16),
            pltpu.VMEM((NF, ROWS, 128), BF16),
            pltpu.VMEM((NX * NH, ROWS, SIDE), BF16),
            pltpu.VMEM((NW, 16, SIDE), BF16),
            pltpu.VMEM((NW, 16, SIDE), BF16),
            pltpu.VMEM((NW, 16, SIDE), BF16),
            pltpu.VMEM((NW, 16, SIDE), BF16),
            pltpu.VMEM((16, SIDE), F32),
            pltpu.VMEM((16, SIDE), F32),
            dma((6,)), dma, dma, dma, pltpu.SemaphoreType.REGULAR, dma, dma, dma, dma, dma, dma, dma, dma,
            pltpu.SemaphoreType.REGULAR, pltpu.SemaphoreType.REGULAR,
            dma, dma, dma, dma,
        ],
        compiler_params=pltpu.CompilerParams(collective_id=0, has_side_effects=True),
    )(strain, inv_asd, spectra, cutoff, jnp.asarray(high), jnp.asarray(low))
    return pl.pallas_call(
        store,
        out_shape=(
            jax.ShapeDtypeStruct((TEMPL, 2, ROWS, SIDE), F32),
            jax.ShapeDtypeStruct((ROWS, SIDE), F32),
        ),
        in_specs=[anywhere, anywhere],
        out_specs=(anywhere, anywhere),
        scratch_shapes=[dma((2,))],
    )(pltpu.with_memory_space_constraint(series, pltpu.VMEM), pltpu.with_memory_space_constraint(peak, pltpu.VMEM))


def solution(mesh):
    in_specs = (P("freq", None), P("freq", None), P("freq", "tmpl", None, None), P("tmpl"))
    out_specs = (P("tmpl", None, "freq", None), P("freq", None))
    return jax.shard_map(local, mesh=mesh, in_specs=in_specs, out_specs=out_specs, check_vma=False)
```

```python
import functools
import math

import jax
import jax.numpy as jnp
import numpy as np
from jax import lax
from jax.experimental import pallas as pl
from jax.experimental.pallas import tpu as pltpu
from jax.sharding import PartitionSpec as P

SIDE = 512
BAND = 256
TOTAL = SIDE * SIDE
NZ = 8
NY = 4
NC = 2
NW = NY * NC
NX = 4
NH = 2
NF = NZ * NW
ROWS = SIDE // NF
TEMPL = 8
PAIRS = 2 * TEMPL
EARLY = NZ // 2
MESH = pl.DeviceIdType.MESH
F32 = jnp.float32
BF16 = jnp.bfloat16


def base_tables():
    index = np.arange(SIDE)
    angle = 2.0 * np.pi / SIDE * (np.outer(index, index) % SIDE)
    cosines = np.cos(angle).astype(np.float32)
    sines = np.sin(angle).astype(np.float32)
    whole = np.concatenate([cosines, sines], 1)
    high = whole.astype(jnp.bfloat16)
    part = np.concatenate([cosines[:, :BAND], sines[:, :BAND]], 1)
    low = (part - part.astype(jnp.bfloat16).astype(np.float32)).astype(jnp.bfloat16)
    return high, low


def iota(shape, axis):
    return lax.broadcasted_iota(jnp.int32, shape, axis)


def dot(left, right):
    return jnp.dot(left, right, preferred_element_type=F32)


def split(value):
    high = value.astype(BF16)
    return high, (value - high.astype(F32)).astype(BF16)


def regroup(values):
    lane = iota((ROWS, 128), 1)
    for bit in range(4):
        low = 1 << bit
        width = ROWS * low
        keep = (lane & width) == 0
        moved = list(values)
        for first in range(PAIRS):
            if first & low:
                continue
            second = first | low
            moved[first] = jnp.where(keep, values[first], pltpu.roll(values[second], width, 1))
            moved[second] = jnp.where(keep, pltpu.roll(values[first], 128 - width, 1), values[second])
        values = moved
    return values


def kernel(
    strain, inv_asd, spectra, cutoff, high_table, low_table, series, peak,
    table, table_low, strain_v, asd_v, spectra_v, cut_s, gathered, partial, partials,
    weights, outgoing, received, bests, mirror_out, mirror_in, early_out, early_in, early_sum, mirror_sum,
    load_sem, z_send, early_recv, late_recv, late_sem, o_send, o_recv, e_send, e_recv, m_send, m_recv, w_send, w_recv, done_sem, ready_sem, f_send, f_recv, t_send, t_recv,
):
    me_t = lax.axis_index("tmpl")
    me_f = lax.axis_index("freq")
    z_pos = me_f // NW
    w_pos = me_f % NW
    core = me_f % NC
    x_pos = me_t // NH
    half = me_t % NH
    y_full = half * NY + w_pos // NC

    loads = [
        pltpu.make_async_copy(strain, strain_v, load_sem.at[0]),
        pltpu.make_async_copy(spectra.at[:, :, :, pl.ds(0, BAND)], spectra_v, load_sem.at[1]),
        pltpu.make_async_copy(inv_asd.at[:, pl.ds(0, BAND)], asd_v, load_sem.at[2]),
        pltpu.make_async_copy(cutoff, cut_s, load_sem.at[3]),
        pltpu.make_async_copy(high_table, table, load_sem.at[4]),
        pltpu.make_async_copy(low_table, table_low, load_sem.at[5]),
    ]
    for load in loads:
        load.start()

    barrier = pltpu.get_barrier_semaphore()

    def greet(device):
        pl.semaphore_signal(barrier, inc=1, device_id=device, device_id_type=MESH)

    early = z_pos < EARLY
    late = jnp.logical_not(early)
    mirror = NZ - 1 - z_pos
    base_z = z_pos // EARLY * EARLY
    for away in (3, 5):
        place = (y_full + away) % (NH * NY)
        for to_core in range(NC):
            greet((x_pos * NH + place // NY, z_pos * NW + place % NY * NC + to_core))
    for step in (3, 1, 2):
        greet((me_t, (base_z + (z_pos + step) % EARLY) * NW + w_pos))

    @pl.when(early)
    def _():
        for late_z in range(EARLY, NZ):
            greet((me_t, late_z * NW + w_pos))

    for away in (2, 6, 1, 7):
        place = (y_full + away) % (NH * NY)
        for to_core in range(NC):
            greet((x_pos * NH + place // NY, z_pos * NW + place % NY * NC + to_core))
    greet((me_t, me_f + 1 - 2 * core))
    for step in (2, 1, 3):
        greet(((x_pos + step) % NX * NH + half, me_f))

    loads[0].wait()
    own = strain_v[...]
    gathered[z_pos] = jnp.concatenate([own[:, :BAND], own[:, BAND:]], 0).astype(BF16)

    alike = EARLY - 1 + (NH * NY - 2) * NC + 1 + NX - 1

    def give(to_z, recv_sem):
        pltpu.make_async_remote_copy(
            src_ref=gathered.at[z_pos], dst_ref=gathered.at[z_pos], send_sem=z_send, recv_sem=recv_sem,
            device_id=(me_t, to_z * NW + w_pos), device_id_type=MESH,
        ).start()

    def arrived(count, sem):
        pltpu.make_async_copy(gathered.at[pl.ds(0, count)], gathered.at[pl.ds(0, count)], sem).wait()

    def tell_line():
        for step in range(1, NW):
            pl.semaphore_signal(
                done_sem, inc=1, device_id=(me_t, z_pos * NW + (w_pos + step) % NW), device_id_type=MESH
            )

    def first_table(z_rows, z_first):
        row = iota((128, 64), 0)
        col = iota((128, 64), 1)
        freq_row = 64 * z_rows + 8 * (row // 16) + row % 8
        sample_row = 64 * (z_first + col // 16) + 8 * w_pos + col % 8
        turns = (freq_row * sample_row + 128 * (row // 8 % 2)) & (SIDE - 1)
        values = jnp.cos(turns.astype(F32) * (2.0 * math.pi / SIDE))
        side = col // 8 % 2
        return jnp.concatenate([jnp.where(side == 0, values, 0.0), jnp.where(side == 1, values, 0.0)], 0)

    def to_group(source, target, send_sem, recv_sem):
        for step, to_core in ((2, 0), (2, 1), (1, 0), (1, 1), (3, 0), (3, 1), (0, 1)):
            if step == 2:
                place = (y_full + (2 if to_core == 0 else 6)) % (NH * NY)
            else:
                place = (y_full + (0, 1, 0, 7)[step]) % (NH * NY)
            target_w = place % NY * NC + (1 - core if step == 0 else to_core)
            pltpu.make_async_remote_copy(
                src_ref=source.at[target_w], dst_ref=target.at[w_pos], send_sem=send_sem, recv_sem=recv_sem,
                device_id=(x_pos * NH + place // NY, z_pos * NW + target_w), device_id_type=MESH,
            ).start()
        target[w_pos] = source[w_pos]

    def first_share(tables, first_z, out):
        blocks = gathered[first_z : first_z + EARLY].reshape(64, BAND)
        shares = dot(tables[0], blocks) + dot(tables[1], blocks)
        out[:, :, :BAND] = shares[:128].reshape(NW, 16, BAND).astype(BF16)
        out[:, :, BAND:] = shares[128:].reshape(NW, 16, BAND).astype(BF16)

    def total(ref):
        sums = ref[0].astype(F32)
        for slot in range(1, NW):
            sums = sums + ref[slot].astype(F32)
        return sums

    def came(ref, sem):
        pltpu.make_async_copy(ref.at[pl.ds(0, NW - 1)], ref.at[pl.ds(0, NW - 1)], sem).wait()

    @pl.when(late)
    def _():
        pl.semaphore_wait(barrier, alike + EARLY)
        for step in (3, 1, 2):
            give(EARLY + (z_pos + step) % EARLY, late_recv)
        for to_z in range(EARLY):
            give(to_z, late_recv)
        pl.semaphore_signal(late_sem, inc=1, device_id=(me_t, mirror * NW + w_pos), device_id_type=MESH)
        tell_line()

    @pl.when(early)
    def _():
        pl.semaphore_wait(barrier, alike)
        for step in (3, 1, 2):
            give((z_pos + step) % EARLY, early_recv)
        mirror_tables = split(first_table(mirror, 0))
        own_tables = split(first_table(z_pos, 0))
        arrived(EARLY - 1, early_recv)
        first_share(mirror_tables, 0, mirror_out)
        to_group(mirror_out, mirror_in, o_send, o_recv)
        first_share(own_tables, 0, early_out)
        to_group(early_out, early_in, e_send, e_recv)

    row = iota((128, 128), 0)
    col = iota((128, 128), 1)
    late_tables = split(first_table(z_pos, EARLY))
    twist = (ROWS * me_f + iota((ROWS, SIDE), 0)) * iota((ROWS, SIDE), 1)
    twist = twist.astype(F32) * (2.0 * math.pi / TOTAL)
    twist_cos = jnp.cos(twist)
    twist_sin = jnp.sin(twist)

    loads[1].wait()
    loads[2].wait()
    loads[3].wait()
    wanted = row % 8 * PAIRS + row // 8 % 8 * 2 + row // 64
    order = jnp.where(col == wanted, 1.0, 0.0).astype(BF16)
    sorted_spectra = dot(order, spectra_v[...].reshape(128, BAND))
    scale = asd_v[...]
    lane = iota((ROWS, BAND), 1)
    for templ in range(TEMPL):
        gain = jnp.where(lane < cut_s[templ], scale, 0.0)
        for part in range(2):
            block = slice((part * TEMPL + templ) * ROWS, (part * TEMPL + templ + 1) * ROWS)
            weights[block, :] = sorted_spectra[block, :] * gain

    @pl.when(early)
    def _():
        came(mirror_in, o_recv)
        mirror_sum[...] = total(mirror_in)
        pl.semaphore_wait(late_sem, 1)
        pltpu.make_async_remote_copy(
            src_ref=mirror_sum, dst_ref=early_sum, send_sem=m_send, recv_sem=m_recv,
            device_id=(me_t, mirror * NW + w_pos), device_id_type=MESH,
        ).start()
        arrived(EARLY, late_recv)

    @pl.when(late)
    def _():
        arrived(EARLY - 1, late_recv)

    first_share(late_tables, EARLY, partial)
    to_group(partial, partials, w_send, w_recv)

    @pl.when(early)
    def _():
        tell_line()
        came(early_in, e_recv)
        early_sum[...] = total(early_in)

    @pl.when(late)
    def _():
        pltpu.make_async_copy(mirror_sum, early_sum, m_recv).wait()

    came(partials, w_recv)
    for step in range(1, NX):
        pl.semaphore_signal(
            ready_sem, inc=1, device_id=((x_pos + step) % NX * NH + half, me_f), device_id_type=MESH
        )
    sums = early_sum[...] + total(partials)
    sum_real = sums[:ROWS]
    sum_imag = sums[ROWS:]
    turned = jnp.concatenate(
        [sum_real * twist_cos + sum_imag * twist_sin, sum_imag * twist_cos - sum_real * twist_sin], 0
    )
    turned_high, turned_low = split(turned)

    loads[4].wait()
    loads[5].wait()
    both = jnp.concatenate([turned_high, turned_low], 0)
    by_cos = dot(both, table[:, :BAND])
    by_sin = dot(both, table[:, SIDE : SIDE + BAND])
    by_cos = by_cos[:16] + by_cos[16:] + dot(turned_high, table_low[:, :BAND])
    by_sin = by_sin[:16] + by_sin[16:] + dot(turned_high, table_low[:, BAND:])
    spec_real = by_cos[:ROWS] + by_sin[ROWS:]
    spec_imag = by_cos[ROWS:] - by_sin[:ROWS]

    product = []
    for templ in range(TEMPL):
        gain_real = weights[templ * ROWS : (templ + 1) * ROWS, :]
        gain_imag = weights[(TEMPL + templ) * ROWS : (TEMPL + templ + 1) * ROWS, :]
        product.append(spec_real * gain_real + spec_imag * gain_imag)
    for templ in range(TEMPL):
        gain_real = weights[templ * ROWS : (templ + 1) * ROWS, :]
        gain_imag = weights[(TEMPL + templ) * ROWS : (TEMPL + templ + 1) * ROWS, :]
        product.append(spec_imag * gain_real - spec_real * gain_imag)
    product = jnp.concatenate(product, 0).astype(BF16)

    def send(target):
        pltpu.make_async_remote_copy(
            src_ref=outgoing.at[target], dst_ref=received.at[me_f], send_sem=f_send, recv_sem=f_recv,
            device_id=(me_t, target), device_id_type=MESH,
        ).start()

    for column, target_zs in ((0, (0, 1)), (1, (2, 3)), (3, (7, 6)), (2, (4, 5))):
        start = column * 128
        by_cos = dot(product, table[:BAND, start : start + 128])
        by_sin = dot(product, table[:BAND, SIDE + start : SIDE + start + 128])
        cos_here = twist_cos[:, start : start + 128]
        sin_here = twist_sin[:, start : start + 128]
        reals = []
        imags = []
        for templ in range(TEMPL):
            up = slice(templ * ROWS, (templ + 1) * ROWS)
            down = slice((TEMPL + templ) * ROWS, (TEMPL + templ + 1) * ROWS)
            real_part = by_cos[up] - by_sin[down]
            imag_part = by_sin[up] + by_cos[down]
            reals.append(real_part * cos_here - imag_part * sin_here)
            imags.append(real_part * sin_here + imag_part * cos_here)
        for slot, tile in enumerate(regroup(reals + imags)):
            outgoing[column * 16 + slot] = tile.astype(BF16)
        if column == 0:
            pl.semaphore_wait(done_sem, NW - 1)
        for target_z in target_zs:

            def send_row(step, carry, target_z=target_z):
                target = target_z * NW + (w_pos + step) % NW
                pl.when(target != me_f)(functools.partial(send, target))
                return carry

            lax.fori_loop(0, NW, send_row, 0)

    received[me_f] = outgoing[me_f]
    pltpu.make_async_copy(received.at[pl.ds(0, NF - 1)], received.at[pl.ds(0, NF - 1)], f_recv).wait()

    columns_in = jnp.transpose(received[...].reshape(SIDE, 128))
    for pair in range(2):
        start = pair * 256
        by_cos = dot(columns_in, table[:, start : start + 256]) * (1.0 / TOTAL)
        by_sin = dot(columns_in, table[:, SIDE + start : SIDE + start + 256]) * (1.0 / TOTAL)
        top = None
        for templ in range(TEMPL):
            up = slice(templ * ROWS, (templ + 1) * ROWS)
            down = slice((TEMPL + templ) * ROWS, (TEMPL + templ + 1) * ROWS)
            real_part = by_cos[up] - by_sin[down]
            imag_part = by_sin[up] + by_cos[down]
            series[templ, 0, :, start : start + 256] = real_part
            series[templ, 1, :, start : start + 256] = imag_part
            power = real_part * real_part + imag_part * imag_part
            top = power if top is None else jnp.maximum(top, power)
        bests[me_t, :, start : start + 256] = top.astype(BF16)

    pl.semaphore_wait(ready_sem, NX - 1)
    for away in ((2, 1), (1, 1), (3, 1), (0, 1), (2, 0), (1, 0), (3, 0)):
        pltpu.make_async_remote_copy(
            src_ref=bests.at[me_t], dst_ref=bests.at[me_t], send_sem=t_send, recv_sem=t_recv,
            device_id=((x_pos + away[0]) % NX * NH + (half + away[1]) % NH, me_f), device_id_type=MESH,
        ).start()
    others = NX * NH - 1
    pltpu.make_async_copy(bests.at[pl.ds(0, others)], bests.at[pl.ds(0, others)], t_recv).wait()
    tops = [bests[slot].astype(F32) for slot in range(NX * NH)]
    while len(tops) > 1:
        tops = [jnp.maximum(tops[i], tops[i + 1]) for i in range(0, len(tops), 2)]
    peak[...] = tops[0]

    @pl.when(early)
    def _():
        arrived(EARLY - 1, z_send)
        came(mirror_out, o_send)
        came(early_out, e_send)
        pltpu.make_async_copy(mirror_sum, early_sum, m_send).wait()

    @pl.when(late)
    def _():
        arrived(NZ - 1, z_send)

    came(partial, w_send)
    pltpu.make_async_copy(outgoing.at[pl.ds(0, NF - 1)], outgoing.at[pl.ds(0, NF - 1)], f_send).wait()
    pltpu.make_async_copy(bests.at[pl.ds(0, others)], bests.at[pl.ds(0, others)], t_send).wait()


def store(series_v, peak_v, series, peak, sems):
    copies = [
        pltpu.make_async_copy(series_v, series, sems.at[0]),
        pltpu.make_async_copy(peak_v, peak, sems.at[1]),
    ]
    for copy in copies:
        copy.start()
    for copy in copies:
        copy.wait()


def local(strain, inv_asd, spectra, cutoff):
    high, low = base_tables()
    anywhere = pl.BlockSpec(memory_space=pl.ANY)
    inside = pl.BlockSpec(memory_space=pltpu.VMEM)
    dma = pltpu.SemaphoreType.DMA
    series, peak = pl.pallas_call(
        kernel,
        out_shape=(
            pltpu.VMEM((TEMPL, 2, ROWS, SIDE), F32),
            pltpu.VMEM((ROWS, SIDE), F32),
        ),
        in_specs=[anywhere] * 6,
        out_specs=(inside, inside),
        scratch_shapes=[
            pltpu.VMEM((SIDE, 2 * SIDE), BF16),
            pltpu.VMEM((SIDE, SIDE), BF16),
            pltpu.VMEM((ROWS, SIDE), F32),
            pltpu.VMEM((ROWS, BAND), F32),
            pltpu.VMEM((ROWS, TEMPL, 2, BAND), BF16),
            pltpu.SMEM((TEMPL,), jnp.int32),
            pltpu.VMEM((NZ, 16, BAND), BF16),
            pltpu.VMEM((NW, 16, SIDE), BF16),
            pltpu.VMEM((NW, 16, SIDE), BF16),
            pltpu.VMEM((128, BAND), F32),
            pltpu.VMEM((NF, ROWS, 128), BF16),
            pltpu.VMEM((NF, ROWS, 128), BF16),
            pltpu.VMEM((NX * NH, ROWS, SIDE), BF16),
            pltpu.VMEM((NW, 16, SIDE), BF16),
            pltpu.VMEM((NW, 16, SIDE), BF16),
            pltpu.VMEM((NW, 16, SIDE), BF16),
            pltpu.VMEM((NW, 16, SIDE), BF16),
            pltpu.VMEM((16, SIDE), F32),
            pltpu.VMEM((16, SIDE), F32),
            dma((6,)), dma, dma, dma, pltpu.SemaphoreType.REGULAR, dma, dma, dma, dma, dma, dma, dma, dma,
            pltpu.SemaphoreType.REGULAR, pltpu.SemaphoreType.REGULAR,
            dma, dma, dma, dma,
        ],
        compiler_params=pltpu.CompilerParams(collective_id=0, has_side_effects=True),
    )(strain, inv_asd, spectra, cutoff, jnp.asarray(high), jnp.asarray(low))
    return pl.pallas_call(
        store,
        out_shape=(
            jax.ShapeDtypeStruct((TEMPL, 2, ROWS, SIDE), F32),
            jax.ShapeDtypeStruct((ROWS, SIDE), F32),
        ),
        in_specs=[anywhere, anywhere],
        out_specs=(anywhere, anywhere),
        scratch_shapes=[dma((2,))],
    )(pltpu.with_memory_space_constraint(series, pltpu.VMEM), pltpu.with_memory_space_constraint(peak, pltpu.VMEM))


def solution(mesh):
    in_specs = (P("freq", None), P("freq", None), P("freq", "tmpl", None, None), P("tmpl"))
    out_specs = (P("tmpl", None, "freq", None), P("freq", None))
    return jax.shard_map(local, mesh=mesh, in_specs=in_specs, out_specs=out_specs, check_vma=False)
```
